32 devices in a mesh: groups: 2 (over x), row: 16 (over z, y, core).
Axes of the slice: x: 2, y: 2, z: 4, core: 2. Of those that a mesh axis runs over, the one named last changes fastest.
Arguments:
- design_matrix: bfloat16 [1024, 65536], P('groups', 'row'), parts along dimension 0, may hold values from -0.0546875 to 0.0546875
- targets: float32 [1024, 128], P(('groups', 'row')), parts along dimension 0, may hold values from -24 to 24
- linear: float32 [131072, 128], P(('groups', 'row')), parts along dimension 0, may hold values from -24 to 24
- diagonal: float32 [131072], P(('groups', 'row')), parts along dimension 0, may hold values from 0.1 to 2
- lower_code: int32 [131072, 128], P(('groups', 'row')), parts along dimension 0, may hold values from -192 to -17
- upper_code: int32 [131072, 128], P(('groups', 'row')), parts along dimension 0, may hold values from 16 to 191
Outputs:
- box_iterate: float32 [131072, 128], P(('groups', 'row')), parts along dimension 0
- scaled_dual: float32 [131072, 128], P(('groups', 'row')), parts along dimension 0
The draws below stay inside these ranges and needn't reach their ends.
There are 2 independent parts, one for each index of `groups`. The reference program is written for one: setup_inputs(seed, part) draws one part's arguments, and reference() takes and returns one part's arrays. A program takes and returns all parts, laid end to end along the dimension named above; each array names one. Nothing has to cross between parts.
All inputs are finite; a program needn't handle non-finite values.
Results may differ from the reference program's by a relative error of at most 0.00033.
Values may be sent and summed in bfloat16 or wider, within the bound.
A program may use at most 128 MiB of HBM per device.

```python
import math
import jax
import jax.numpy as jnp
from jax import lax

N = 65536
K = 512
S = 128
ITERS = 4
DEPTH = 5


def place_ends(drawn, own_key, least, largest):
    longest = drawn.shape.index(max(drawn.shape))
    spots = []
    for shift in (0, 1):
        where = [jax.random.randint(jax.random.fold_in(own_key, axis), (), 0, length) for axis, length in enumerate(drawn.shape)]
        where[longest] = (where[longest] + shift) % drawn.shape[longest]
        spots.append(tuple(where))
    return drawn.at[spots[0]].set(least).at[spots[1]].set(largest)


def raised(array, key, source, target, shards_of, factor):
    def block_of(position):
        return (jnp.arange(array.shape[position]) // (array.shape[position] // shards_of)).reshape((-1,) + (1,) * (array.ndim - 1 - position))

    near = jax.random.permutation(key, shards_of)[block_of(target)]
    far = (block_of(target) + shards_of // 2) % shards_of
    return jnp.where((block_of(source) == near) | (block_of(source) == far), factor * array, array)


def level_of(key, extent, pieces, smallest, largest):
    loudness = 1.0
    for dim, shards_of in pieces:
        draws = jax.random.uniform(jax.random.fold_in(jax.random.fold_in(key, 6), dim), (shards_of,), jnp.float32, smallest / len(pieces), largest / len(pieces))
        loudness = loudness * jnp.repeat(jnp.exp(draws), extent[dim] // shards_of).reshape((-1,) + (1,) * (len(extent) - 1 - dim))
    return loudness


def gaussian(rng, extent, deviation, bound, shards=(), kind=jnp.bfloat16):
    values = jax.random.normal(rng, extent, jnp.float32) * deviation
    if len(shards) > 0:
        values = level_of(rng, extent, shards, -0.22, 0.18) * values
    return jnp.clip(values, min=-bound, max=bound).astype(kind)


def noise_with(own_key, extent, spread, reach, shards, heavy, held_as=jnp.bfloat16):
    values = spread * jax.random.normal(own_key, extent, jnp.float32)
    if shards:
        values = values * level_of(own_key, extent, shards, -0.22, 0.18)
    return jnp.clip(raised(values, jax.random.fold_in(own_key, 3), *heavy), -reach, reach).astype(held_as)


def setup_inputs(seed: int = 0, part: int = 0) -> dict:
    key_of = jax.random.split(jax.random.key(seed), 7)
    part_keys = jax.random.split(jax.random.fold_in(key_of[6], part), 7)
    design_matrix = noise_with(part_keys[0], (K, N), (max(N // 3, 2 * K)) ** -0.5, 0.0546875, ((1, 16),), (1, 0, 16, 2.0))
    targets = gaussian(part_keys[1], (K, S), 4.0, 24.0, ((0, 16),), jnp.float32)
    linear = gaussian(part_keys[2], (N, S), 4.0, 24.0, ((0, 16),), jnp.float32)
    diagonal = jnp.clip(jnp.exp(math.log(2.0) - 2.9957323 * jax.random.uniform(part_keys[3], (N,), jnp.float32) ** level_of(part_keys[3], (N,), ((0, 16),), -0.2, 0.2)), 0.1, 2.0)
    lower_code = place_ends(jax.random.randint(part_keys[4], (N, S), -192, -16), jax.random.fold_in(part_keys[4], 1), -192, (-16) - 1).astype(jnp.int32)
    upper_code = place_ends(jax.random.randint(part_keys[5], (N, S), 16, 192), jax.random.fold_in(part_keys[5], 1), 16, 191).astype(jnp.int32)
    return {"design_matrix": design_matrix, "targets": targets, "linear": linear, "diagonal": diagonal, "lower_code": lower_code, "upper_code": upper_code}


rho_plus_lip = 7.0


def solve_small(matrix, rhs):
    count = len(rhs)
    table = [list(line) for line in matrix]
    right = list(rhs)
    for p in range(count):
        for i in range(p + 1, count):
            factor = table[i][p] / table[p][p]
            for j in range(p, count):
                table[i][j] = table[i][j] - factor * table[p][j]
            right[i] = right[i] - factor * right[p]
    result = [None] * count
    for i in reversed(range(count)):
        total = right[i]
        for j in range(i + 1, count):
            total = total - table[i][j] * result[j]
        result[i] = total / table[i][i]
    return result


def mix_weights(gram):
    count = len(gram)
    trace = gram[0][0]
    for i in range(1, count):
        trace = trace + gram[i][i]
    shift = 0.01 * trace / count + 1e-6
    matrix = [[gram[i][j] + (shift if i == j else 0.0) for j in range(count)] for i in range(count)]
    solved = solve_small(matrix, [jnp.ones_like(trace)] * count)
    total = solved[0]
    for i in range(1, count):
        total = total + solved[i]
    return [item / total for item in solved]


def reference(design_matrix, targets, linear, diagonal, lower_code, upper_code):
    lower = lower_code.astype(jnp.float32) / 64.0
    upper = upper_code.astype(jnp.float32) / 64.0
    step_size = (1.0 / (rho_plus_lip + diagonal))[:, None]

    def apply_map(state):
        point = state[0] - state[1]
        point_b = point.astype(jnp.bfloat16)
        product = jnp.dot(design_matrix, point_b, preferred_element_type=jnp.float32)
        misfit = (product - targets).astype(jnp.bfloat16)
        gradient = lax.dot_general(design_matrix, misfit, (((0,), (0,)), ((), ())), preferred_element_type=jnp.float32)
        gradient = gradient + diagonal[:, None] * point + linear
        moved = point - step_size * gradient
        boxed = jnp.clip(moved + state[1], lower, upper)
        scaled = state[1] + moved - boxed
        return jnp.stack([boxed, scaled])

    state = jnp.zeros((2,) + linear.shape, jnp.float32)
    hist_mapped = []
    hist_change = []
    for iteration in range(ITERS):
        mapped = apply_map(state)
        hist_mapped.append(mapped)
        hist_change.append(mapped - state)
        if len(hist_mapped) > DEPTH:
            hist_mapped.pop(0)
            hist_change.pop(0)
        stacked = jnp.stack(hist_change)
        whole = jnp.einsum('icns,jcns->ijs', stacked, stacked, precision=lax.Precision.HIGHEST)
        count = len(hist_change)
        gram = [[whole[i, j] for j in range(count)] for i in range(count)]
        alpha = mix_weights(gram)
        combined = alpha[0][None, None, :] * hist_mapped[0]
        for i in range(1, count):
            combined = combined + alpha[i][None, None, :] * hist_mapped[i]
        state = jnp.stack([jnp.clip(combined[0], lower, upper), combined[1]])
    return state[0], state[1]
```

```python
import functools

import jax
import jax.numpy as jnp
from jax import lax
from jax.experimental import pallas as pl
from jax.experimental.pallas import tpu as pltpu
from jax.sharding import PartitionSpec as P

ITERS = 4

rho_plus_lip = 7.0


def solve_small(matrix, rhs):
    count = len(rhs)
    table = [list(line) for line in matrix]
    right = list(rhs)
    for p in range(count):
        for i in range(p + 1, count):
            factor = table[i][p] / table[p][p]
            for j in range(p, count):
                table[i][j] = table[i][j] - factor * table[p][j]
            right[i] = right[i] - factor * right[p]
    result = [None] * count
    for i in reversed(range(count)):
        total = right[i]
        for j in range(i + 1, count):
            total = total - table[i][j] * result[j]
        result[i] = total / table[i][i]
    return result


def mix_weights(gram):
    count = len(gram)
    trace = gram[0][0]
    for i in range(1, count):
        trace = trace + gram[i][i]
    shift = 0.01 * trace / count + 1e-06
    matrix = [[gram[i][j] + (shift if i == j else 0.0) for j in range(count)] for i in range(count)]
    solved = solve_small(matrix, [jnp.ones_like(trace)] * count)
    total = solved[0]
    for i in range(1, count):
        total = total + solved[i]
    return [item / total for item in solved]


def greet(n, me):
    barrier = pltpu.get_barrier_semaphore()
    for d in range(1, n):
        pl.semaphore_signal(
            barrier,
            inc=1,
            device_id={"row": lax.rem(me + d, n)},
            device_id_type=pl.DeviceIdType.MESH,
        )
    pl.semaphore_wait(barrier, n - 1)


def send(src, dst, send_sem, recv_sem, peer):
    copy = pltpu.make_async_remote_copy(
        src_ref=src,
        dst_ref=dst,
        send_sem=send_sem,
        recv_sem=recv_sem,
        device_id={"row": peer},
        device_id_type=pl.DeviceIdType.MESH,
    )
    copy.start()
    return copy


def spread(n, me, mine, whole, send_sem, recv_sem):
    copies = []
    for d in range(1, n):
        copies.append(
            send(mine, whole.at[me], send_sem.at[d], recv_sem.at[d], lax.rem(me + d, n))
        )
    whole[me] = mine[...]
    for copy in copies:
        copy.wait()


def first_misfit_kernel(n, targets_ref, out_ref, mine, whole, send_sem, recv_sem):
    me = lax.axis_index("row")
    mine[...] = (0.0 - targets_ref[...]).astype(jnp.bfloat16)
    greet(n, me)
    spread(n, me, mine, whole, send_sem, recv_sem)
    out_ref[...] = whole[...]


def misfit_kernel(
    n, product_ref, targets_ref, out_ref, slots, mine, whole, send_a, recv_a, send_b, recv_b
):
    me = lax.axis_index("row")
    greet(n, me)
    copies = []
    for d in range(1, n):
        peer = lax.rem(me + d, n)
        copies.append(
            send(product_ref.at[peer], slots.at[d - 1], send_a.at[d], recv_a.at[d], peer)
        )
    total = product_ref[me]
    for d in range(1, n):
        copies[d - 1].wait_recv()
        total = total + slots[d - 1]
    mine[...] = (total - targets_ref[...]).astype(jnp.bfloat16)
    spread(n, me, mine, whole, send_b, recv_b)
    for copy in copies:
        copy.wait_send()
    out_ref[...] = whole[...]


def gram_kernel(n, part_ref, out_ref, whole, send_sem, recv_sem):
    me = lax.axis_index("row")
    greet(n, me)
    spread(n, me, part_ref, whole, send_sem, recv_sem)
    total = whole[0]
    for i in range(1, n):
        total = total + whole[i]
    out_ref[...] = total


VMEM = pl.BlockSpec(memory_space=pltpu.VMEM)


def comm_params(number):
    return pltpu.CompilerParams(collective_id=number, has_side_effects=True)


def first_misfit(n, targets):
    kr, s = targets.shape
    out = pl.pallas_call(
        functools.partial(first_misfit_kernel, n),
        out_shape=jax.ShapeDtypeStruct((n, kr, s), jnp.bfloat16),
        in_specs=[VMEM],
        out_specs=VMEM,
        scratch_shapes=[
            pltpu.VMEM((kr, s), jnp.bfloat16),
            pltpu.VMEM((n, kr, s), jnp.bfloat16),
            pltpu.SemaphoreType.DMA((n,)),
            pltpu.SemaphoreType.DMA((n,)),
        ],
        compiler_params=comm_params(0),
        name="first_misfit",
    )(targets)
    return out.reshape(n * kr, s)


def next_misfit(n, product, targets):
    kr, s = targets.shape
    out = pl.pallas_call(
        functools.partial(misfit_kernel, n),
        out_shape=jax.ShapeDtypeStruct((n, kr, s), jnp.bfloat16),
        in_specs=[VMEM] * 2,
        out_specs=VMEM,
        scratch_shapes=[
            pltpu.VMEM((n - 1, kr, s), jnp.float32),
            pltpu.VMEM((kr, s), jnp.bfloat16),
            pltpu.VMEM((n, kr, s), jnp.bfloat16),
        ]
        + [pltpu.SemaphoreType.DMA((n,))] * 4,
        compiler_params=comm_params(1),
        name="next_misfit",
    )(product.reshape(n, kr, s), targets)
    return out.reshape(n * kr, s)


def sum_gram(n, part):
    return pl.pallas_call(
        functools.partial(gram_kernel, n),
        out_shape=jax.ShapeDtypeStruct(part.shape, part.dtype),
        in_specs=[VMEM],
        out_specs=VMEM,
        scratch_shapes=[
            pltpu.VMEM((n,) + part.shape, part.dtype),
            pltpu.SemaphoreType.DMA((n,)),
            pltpu.SemaphoreType.DMA((n,)),
        ],
        compiler_params=comm_params(2),
        name="sum_gram",
    )(part)


def bounds(lo_ref, hi_ref):
    return (
        lo_ref[...].astype(jnp.float32) * (1.0 / 64.0),
        hi_ref[...].astype(jnp.float32) * (1.0 / 64.0),
    )


def column_sum(x):
    return jnp.sum(x, axis=0, keepdims=True)


def start_kernel(a_ref, mis_ref, lin_ref, diag_ref, lo_ref, hi_ref, z_ref, u_ref, product_ref):
    lower, upper = bounds(lo_ref, hi_ref)
    gradient = lax.dot_general(
        a_ref[...], mis_ref[...], (((0,), (0,)), ((), ())), preferred_element_type=jnp.float32
    )
    gradient = gradient + lin_ref[...]
    moved = 0.0 - (1.0 / (rho_plus_lip + diag_ref[...])) * gradient
    boxed = jnp.minimum(jnp.maximum(moved, lower), upper)
    scaled = moved - boxed
    z_ref[...] = boxed
    u_ref[...] = scaled
    add = jnp.dot(
        a_ref[...], (boxed - scaled).astype(jnp.bfloat16), preferred_element_type=jnp.float32
    )

    @pl.when(pl.program_id(0) == 0)
    def _():
        product_ref[...] = jnp.zeros_like(product_ref)

    product_ref[...] += add


def map_kernel(iteration, *refs):
    a_ref, mis_ref, lin_ref, diag_ref, lo_ref, hi_ref, z_ref, u_ref = refs[:8]
    rest = refs[8:]
    if iteration == 1:
        prior = [(z_ref, u_ref)]
    else:
        prior = [(rest[2 * i], rest[2 * i + 1]) for i in range(iteration)]
        rest = rest[2 * iteration:]
    mz_ref, mu_ref = rest[:2]
    gram_ref = rest[-1]
    lower, upper = bounds(lo_ref, hi_ref)
    z, u = z_ref[...], u_ref[...]
    point = z - u
    diagonal = diag_ref[...]
    gradient = lax.dot_general(
        a_ref[...], mis_ref[...], (((0,), (0,)), ((), ())), preferred_element_type=jnp.float32
    )
    gradient = gradient + diagonal * point + lin_ref[...]
    moved = point - (1.0 / (rho_plus_lip + diagonal)) * gradient
    boxed = jnp.minimum(jnp.maximum(moved + u, lower), upper)
    scaled = u + moved - boxed
    mz_ref[...] = boxed
    mu_ref[...] = scaled
    cz, cu = boxed - z, scaled - u
    if iteration < ITERS - 1:
        rest[2][...] = cz
        rest[3][...] = cu
    rows = [column_sum(cz * pz[...] + cu * pu[...]) for pz, pu in prior]
    rows.append(column_sum(cz * cz + cu * cu))
    if iteration == 1:
        rows.append(column_sum(z * z + u * u))

    @pl.when(pl.program_id(0) == 0)
    def _():
        gram_ref[...] = jnp.zeros_like(gram_ref)

    for i, row in enumerate(rows):
        gram_ref[i:i + 1, :] += row


def mix_kernel(iteration, *refs):
    count = iteration + 1
    grams, refs = refs[:iteration], refs[iteration:]
    lo_ref, hi_ref = refs[:2]
    mapped = [(refs[2 + 2 * i], refs[3 + 2 * i]) for i in range(count)]
    refs = refs[2 + 2 * count:]
    last = iteration == ITERS - 1
    if last:
        z_ref, u_ref, alpha_ref = refs
    else:
        a_ref, z_ref, u_ref, product_ref, alpha_ref = refs

    @pl.when(pl.program_id(0) == 0)
    def _():
        gram = [[None] * count for _ in range(count)]
        gram[0][0] = grams[0][2:3, :]
        for i in range(1, count):
            for j in range(i + 1):
                gram[i][j] = gram[j][i] = grams[i - 1][j:j + 1, :]
        for i, row in enumerate(mix_weights(gram)):
            alpha_ref[i:i + 1, :] = row
        if not last:
            product_ref[...] = jnp.zeros_like(product_ref)

    lower, upper = bounds(lo_ref, hi_ref)
    z = alpha_ref[0:1, :] * mapped[0][0][...]
    u = alpha_ref[0:1, :] * mapped[0][1][...]
    for i in range(1, count):
        z = z + alpha_ref[i:i + 1, :] * mapped[i][0][...]
        u = u + alpha_ref[i:i + 1, :] * mapped[i][1][...]
    z = jnp.minimum(jnp.maximum(z, lower), upper)
    z_ref[...] = z
    u_ref[...] = u
    if not last:
        product_ref[...] += jnp.dot(
            a_ref[...], (z - u).astype(jnp.bfloat16), preferred_element_type=jnp.float32
        )


def per_device(n, design_matrix, targets, linear, diagonal, lower_code, upper_code):
    k, local = design_matrix.shape
    s = linear.shape[1]
    block = min(512, local)
    grid = (local // block,)
    tile = pl.BlockSpec((block, s), lambda i: (i, 0))
    a_spec = pl.BlockSpec((k, block), lambda i: (0, i))
    d_spec = pl.BlockSpec((block, 1), lambda i: (i, 0))
    k_spec = pl.BlockSpec((k, s), lambda i: (0, 0))
    g_spec = pl.BlockSpec((8, s), lambda i: (0, 0))
    big = jax.ShapeDtypeStruct((local, s), jnp.float32)
    tall = jax.ShapeDtypeStruct((k, s), jnp.float32)
    small = jax.ShapeDtypeStruct((8, s), jnp.float32)
    params = pltpu.CompilerParams(dimension_semantics=("arbitrary",))
    diag = diagonal[:, None]

    misfit = first_misfit(n, targets)
    z, u, product = pl.pallas_call(
        start_kernel,
        grid=grid,
        in_specs=[a_spec, k_spec, tile, d_spec, tile, tile],
        out_specs=[tile, tile, k_spec],
        out_shape=[big, big, tall],
        compiler_params=params,
        name="start",
    )(design_matrix, misfit, linear, diag, lower_code, upper_code)
    mapped = [z, u]
    changes = [z, u]
    grams = []
    for iteration in range(1, ITERS):
        last = iteration == ITERS - 1
        misfit = next_misfit(n, product, targets)
        prior = changes if iteration > 1 else []
        out = pl.pallas_call(
            functools.partial(map_kernel, iteration),
            grid=grid,
            in_specs=[a_spec, k_spec, tile, d_spec] + [tile] * (4 + len(prior)),
            out_specs=[tile] * (2 if last else 4) + [g_spec],
            out_shape=[big] * (2 if last else 4) + [small],
            compiler_params=params,
            name="map",
        )(design_matrix, misfit, linear, diag, lower_code, upper_code, z, u, *prior)
        mapped = mapped + list(out[:2])
        changes = changes + list(out[2:-1])
        grams.append(sum_gram(n, out[-1]))
        out = pl.pallas_call(
            functools.partial(mix_kernel, iteration),
            grid=grid,
            in_specs=[g_spec] * iteration
            + [tile] * (2 + len(mapped))
            + ([] if last else [a_spec]),
            out_specs=[tile, tile] + ([] if last else [k_spec]),
            out_shape=[big, big] + ([] if last else [tall]),
            scratch_shapes=[pltpu.VMEM((8, s), jnp.float32)],
            compiler_params=params,
            name="mix",
        )(*grams, lower_code, upper_code, *mapped, *([] if last else [design_matrix]))
        if last:
            z, u = out
        else:
            z, u, product = out
    return z, u


def solution(mesh):
    in_specs = (
        P("groups", "row"),
        P(("groups", "row"), None),
        P(("groups", "row"), None),
        P(("groups", "row")),
        P(("groups", "row"), None),
        P(("groups", "row"), None),
    )
    out_specs = (P(("groups", "row"), None), P(("groups", "row"), None))
    return jax.shard_map(
        functools.partial(per_device, mesh.shape["row"]),
        mesh=mesh,
        in_specs=in_specs,
        out_specs=out_specs,
        check_vma=False,
    )
```

```python
import functools

import jax
import jax.numpy as jnp
from jax import lax
from jax.experimental import pallas as pl
from jax.experimental.pallas import tpu as pltpu
from jax.sharding import PartitionSpec as P

ITERS = 4
TERM = jnp.float32

rho_plus_lip = 7.0


def solve_small(matrix, rhs):
    count = len(rhs)
    table = [list(line) for line in matrix]
    right = list(rhs)
    for p in range(count):
        for i in range(p + 1, count):
            factor = table[i][p] / table[p][p]
            for j in range(p, count):
                table[i][j] = table[i][j] - factor * table[p][j]
            right[i] = right[i] - factor * right[p]
    result = [None] * count
    for i in reversed(range(count)):
        total = right[i]
        for j in range(i + 1, count):
            total = total - table[i][j] * result[j]
        result[i] = total / table[i][i]
    return result


def mix_weights(gram):
    count = len(gram)
    trace = gram[0][0]
    for i in range(1, count):
        trace = trace + gram[i][i]
    shift = 0.01 * trace / count + 1e-06
    matrix = [[gram[i][j] + (shift if i == j else 0.0) for j in range(count)] for i in range(count)]
    solved = solve_small(matrix, [jnp.ones_like(trace)] * count)
    total = solved[0]
    for i in range(1, count):
        total = total + solved[i]
    return [item / total for item in solved]


def greet(n, me):
    barrier = pltpu.get_barrier_semaphore()
    for d in range(1, n):
        pl.semaphore_signal(
            barrier,
            inc=1,
            device_id={"row": lax.rem(me + d, n)},
            device_id_type=pl.DeviceIdType.MESH,
        )
    pl.semaphore_wait(barrier, n - 1)


def send(src, dst, send_sem, recv_sem, peer):
    copy = pltpu.make_async_remote_copy(
        src_ref=src,
        dst_ref=dst,
        send_sem=send_sem,
        recv_sem=recv_sem,
        device_id={"row": peer},
        device_id_type=pl.DeviceIdType.MESH,
    )
    copy.start()
    return copy


def spread(n, me, mine, whole, send_sem, recv_sem):
    copies = []
    for d in range(1, n):
        copies.append(
            send(mine, whole.at[me], send_sem.at[d], recv_sem.at[d], lax.rem(me + d, n))
        )
    whole[me] = mine[...]
    for copy in copies:
        copy.wait()


def chunks(local, size, body):
    def step(i, carry):
        body(pl.ds(pl.multiple_of(i * size, size), size))
        return carry

    lax.fori_loop(0, local // size, step, 0)


def column_sum(x):
    return jnp.sum(x, axis=0, keepdims=True)


def clip_codes(x, lo_ref, hi_ref, at):
    lower = lo_ref[at, :].astype(jnp.float32) * (1.0 / 64.0)
    upper = hi_ref[at, :].astype(jnp.float32) * (1.0 / 64.0)
    return jnp.minimum(jnp.maximum(x, lower), upper)


def whole_kernel(
    n,
    size,
    a_ref,
    targets_ref,
    lin_ref,
    diag_ref,
    lo_ref,
    hi_ref,
    z_ref,
    u_ref,
    mapped,
    changes,
    acc,
    terms,
    slots,
    mine,
    misfits,
    part,
    parts,
    grams,
    alpha_ref,
    send_a,
    recv_a,
    send_b,
    recv_b,
    send_c,
    recv_c,
):
    me = lax.axis_index("row")
    local = lin_ref.shape[0]
    k = a_ref.shape[0]

    def gradient_of(at):
        return lax.dot_general(
            a_ref[:, at],
            misfits[...].reshape(k, -1),
            (((0,), (0,)), ((), ())),
            preferred_element_type=jnp.float32,
        )

    def add_product(at, point):
        acc[...] += jnp.dot(
            a_ref[:, at], point.astype(jnp.bfloat16), preferred_element_type=jnp.float32
        )

    mine[...] = (0.0 - targets_ref[...]).astype(jnp.bfloat16)
    greet(n, me)
    spread(n, me, mine, misfits, send_b, recv_b)
    acc[...] = jnp.zeros_like(acc)
    part[...] = jnp.zeros_like(part)

    def start(at):
        gradient = gradient_of(at) + lin_ref[at, :]
        moved = 0.0 - (1.0 / (rho_plus_lip + diag_ref[at, :])) * gradient
        boxed = clip_codes(moved, lo_ref, hi_ref, at)
        scaled = moved - boxed
        mapped[0, 0, at, :] = boxed
        mapped[0, 1, at, :] = scaled
        part[7:8, :] += column_sum(boxed * boxed + scaled * scaled)
        add_product(at, boxed - scaled)

    chunks(local, size, start)

    for iteration in range(1, ITERS):
        count = iteration + 1
        last = iteration == ITERS - 1
        terms[...] = acc[...].reshape(terms.shape).astype(terms.dtype)
        copies = []
        for d in range(1, n):
            peer = lax.rem(me + d, n)
            copies.append(
                send(terms.at[peer], slots.at[d - 1], send_a.at[d], recv_a.at[d], peer)
            )
        total = terms[me].astype(jnp.float32)
        for d in range(1, n):
            copies[d - 1].wait_recv()
            total = total + slots[d - 1].astype(jnp.float32)
        mine[...] = (total - targets_ref[...]).astype(jnp.bfloat16)
        spread(n, me, mine, misfits, send_b, recv_b)
        for copy in copies:
            copy.wait_send()
        if iteration > 1:
            part[...] = jnp.zeros_like(part)

        def advance(at):
            if iteration == 1:
                z, u = mapped[0, 0, at, :], mapped[0, 1, at, :]
            else:
                z, u = z_ref[at, :], u_ref[at, :]
            point = z - u
            diagonal = diag_ref[at, :]
            gradient = gradient_of(at) + diagonal * point + lin_ref[at, :]
            moved = point - (1.0 / (rho_plus_lip + diagonal)) * gradient
            boxed = clip_codes(moved + u, lo_ref, hi_ref, at)
            scaled = u + moved - boxed
            mapped[iteration, 0, at, :] = boxed
            mapped[iteration, 1, at, :] = scaled
            cz, cu = boxed - z, scaled - u
            if not last:
                changes[iteration - 1, 0, at, :] = cz
                changes[iteration - 1, 1, at, :] = cu
            part[0:1, :] += column_sum(cz * mapped[0, 0, at, :] + cu * mapped[0, 1, at, :])
            for i in range(1, iteration):
                part[i:i + 1, :] += column_sum(
                    cz * changes[i - 1, 0, at, :] + cu * changes[i - 1, 1, at, :]
                )
            part[iteration:count, :] += column_sum(cz * cz + cu * cu)

        chunks(local, size, advance)

        spread(n, me, part, parts, send_c, recv_c)
        whole = parts[0]
        for i in range(1, n):
            whole = whole + parts[i]
        grams[iteration - 1] = whole

        gram = [[None] * count for _ in range(count)]
        gram[0][0] = grams[0, 7:8, :]
        for i in range(1, count):
            for j in range(i + 1):
                gram[i][j] = gram[j][i] = grams[i - 1, j:j + 1, :]
        for i, row in enumerate(mix_weights(gram)):
            alpha_ref[i:i + 1, :] = row
        acc[...] = jnp.zeros_like(acc)

        def mix(at):
            z = alpha_ref[0:1, :] * mapped[0, 0, at, :]
            u = alpha_ref[0:1, :] * mapped[0, 1, at, :]
            for i in range(1, count):
                z = z + alpha_ref[i:i + 1, :] * mapped[i, 0, at, :]
                u = u + alpha_ref[i:i + 1, :] * mapped[i, 1, at, :]
            z = clip_codes(z, lo_ref, hi_ref, at)
            z_ref[at, :] = z
            u_ref[at, :] = u
            if not last:
                add_product(at, z - u)

        chunks(local, size, mix)


def per_device(n, design_matrix, targets, linear, diagonal, lower_code, upper_code):
    k = design_matrix.shape[0]
    local, s = linear.shape
    kr = k // n
    big = jax.ShapeDtypeStruct((local, s), jnp.float32)
    vmem = pl.BlockSpec(memory_space=pltpu.VMEM)
    dma = pltpu.SemaphoreType.DMA((n,))
    return pl.pallas_call(
        functools.partial(whole_kernel, n, min(512, local)),
        in_specs=[vmem] * 6,
        out_specs=[vmem] * 2,
        out_shape=[big, big],
        scratch_shapes=[
            pltpu.VMEM((ITERS, 2, local, s), jnp.float32),
            pltpu.VMEM((ITERS - 2, 2, local, s), jnp.float32),
            pltpu.VMEM((k, s), jnp.float32),
            pltpu.VMEM((n, kr, s), TERM),
            pltpu.VMEM((n - 1, kr, s), TERM),
            pltpu.VMEM((kr, s), jnp.bfloat16),
            pltpu.VMEM((n, kr, s), jnp.bfloat16),
            pltpu.VMEM((8, s), jnp.float32),
            pltpu.VMEM((n, 8, s), jnp.float32),
            pltpu.VMEM((ITERS - 1, 8, s), jnp.float32),
            pltpu.VMEM((8, s), jnp.float32),
        ]
        + [dma] * 6,
        compiler_params=pltpu.CompilerParams(
            collective_id=0, has_side_effects=True, vmem_limit_bytes=60 * 1024 * 1024
        ),
        name="whole",
    )(design_matrix, targets, linear, diagonal[:, None], lower_code, upper_code)


def solution(mesh):
    in_specs = (
        P("groups", "row"),
        P(("groups", "row"), None),
        P(("groups", "row"), None),
        P(("groups", "row")),
        P(("groups", "row"), None),
        P(("groups", "row"), None),
    )
    out_specs = (P(("groups", "row"), None), P(("groups", "row"), None))
    return jax.shard_map(
        functools.partial(per_device, mesh.shape["row"]),
        mesh=mesh,
        in_specs=in_specs,
        out_specs=out_specs,
        check_vma=False,
    )
```
